128 devices in a mesh: section: 4 (over z), seq: 32 (over y, x, core).
Axes of the slice: x: 4, y: 4, z: 4, core: 2. Of those that a mesh axis runs over, the one named last changes fastest.
Arguments:
- tokens: bfloat16 [4, 256, 8192], P('section', 'seq'), may hold values from -6 to 6
- norm_gain: bfloat16 [4, 8192], P('section'), may hold values from 0.099609375 to 1.8984375
- w_query: bfloat16 [4, 8192, 8192], P('section', None, 'seq'), may hold values from -0.0625 to 0.0625
- key_projection: bfloat16 [4, 8192, 1024], P('section', None, 'seq'), may hold values from -0.1875 to 0.1875
- value_projection: bfloat16 [4, 8192, 1024], P('section', None, 'seq'), may hold values from -0.0625 to 0.0625
- w_out: bfloat16 [4, 8192, 8192], P('section', 'seq'), may hold values from -0.0625 to 0.0625
- key_cache: bfloat16 [4, 65536, 8, 128], P('section', 'seq'), may hold values from -400 to 400
- cached_value_rows: bfloat16 [4, 65536, 8, 128], P('section', 'seq'), may hold values from -6 to 6
- cache_mask: int32 [4, 8, 512], P('section', None, 'seq'), may hold values 0 or 1
- span_offset: int32 [4], P('section'), may hold values from 0 to 32767
Outputs:
- handed: bfloat16 [4, 256, 8192], P('section', 'seq')
The draws below stay inside these ranges and needn't reach their ends.
All inputs are finite; a program needn't handle non-finite values. No bound on the sum of `cache_mask` on one device may be relied on, other than what follows from the above.
Results may differ from the reference program's by a relative error of at most 0.014.
Values may be sent and summed in bfloat16 or wider, within the bound.
A program may use at most 192 MiB of HBM per device.

```python
import jax
import jax.numpy as jnp
from jax import lax

MODEL_WIDTH = 8192
HQ = 64
KEY_VALUE_HEADS = 8
HEAD_SIZE = 128
GROUP = 8
QB = 32
KB = 128
RELAY_SECTIONS = 4
SECTION_TOKENS = 256
CONTEXT_LENGTH = 65536
NQB = 8
NKB = 512


def draw_key_cache(key, part):
    first = jax.random.fold_in(key, 0)
    array_shape = (RELAY_SECTIONS, CONTEXT_LENGTH, KEY_VALUE_HEADS, HEAD_SIZE)
    values = 2.2 * jnp.clip(jax.random.normal(first, array_shape, jnp.float32), -6.0, 6.0)
    return values.astype(jnp.bfloat16)


def plant(entries, own_key, smallest, high):
    shape = entries.shape
    index_at = [jax.random.randint(jax.random.fold_in(own_key, axis), (), 0, shape[axis]) for axis in range(len(shape))]
    entries = entries.at[tuple(index_at)].set(smallest)
    longest = shape.index(max(shape))
    index_at[longest] = (index_at[longest] + 1) % shape[longest]
    return entries.at[tuple(index_at)].set(high)


def level_of(rng, shape, cuts, low, high):
    level, own = 1.0, jax.random.fold_in(rng, 6)
    for axis_at, blocks in cuts:
        steps = jnp.exp(jax.random.uniform(jax.random.fold_in(own, axis_at), (blocks,), jnp.float32, low / len(cuts), high / len(cuts)))
        level = level * jnp.repeat(steps, shape[axis_at] // blocks).reshape([-1 if axis == axis_at else 1 for axis in range(len(shape))])
    return level


def gaussian(stream_key, dims, width, reach, cuts=(), kind=jnp.bfloat16):
    level = level_of(stream_key, dims, cuts, -0.22, 0.18) if cuts else 1.0
    entries = jax.random.normal(stream_key, dims, jnp.float32) * width * level
    return jnp.minimum(jnp.maximum(entries, -reach), reach).astype(kind)


def setup_inputs(seed: int = 0) -> dict:
    streams_of = jax.random.split(jax.random.key(seed), 11)
    return {
        "tokens": gaussian(streams_of[0], (RELAY_SECTIONS, SECTION_TOKENS, MODEL_WIDTH), 1.0, 6.0, ((0, 4), (1, 32))),
        "norm_gain": jnp.clip(1.0 + 0.18 * jax.random.normal(streams_of[1], (RELAY_SECTIONS, MODEL_WIDTH), jnp.float32), 0.099609375, 1.8984375).astype(jnp.bfloat16),
        "w_query": gaussian(streams_of[2], (RELAY_SECTIONS, MODEL_WIDTH, HQ * HEAD_SIZE), MODEL_WIDTH ** -0.5, 0.0625, ((0, 4), (2, 32))),
        "key_projection": gaussian(streams_of[3], (RELAY_SECTIONS, MODEL_WIDTH, KEY_VALUE_HEADS * HEAD_SIZE), (MODEL_WIDTH // 9) ** -0.5, 0.1875, ((0, 4), (2, 32))),
        "value_projection": gaussian(streams_of[4], (RELAY_SECTIONS, MODEL_WIDTH, KEY_VALUE_HEADS * HEAD_SIZE), MODEL_WIDTH ** -0.5, 0.0625, ((0, 4), (2, 32))),
        "w_out": gaussian(streams_of[5], (RELAY_SECTIONS, HQ * HEAD_SIZE, MODEL_WIDTH), (HQ * HEAD_SIZE) ** -0.5, 0.0625, ((0, 4), (1, 32))),
        "key_cache": draw_key_cache(jax.random.fold_in(streams_of[10], 71), 0),
        "cached_value_rows": gaussian(streams_of[7], (RELAY_SECTIONS, CONTEXT_LENGTH, KEY_VALUE_HEADS, HEAD_SIZE), 1.0, 6.0, ((0, 4), (1, 32))),
        "cache_mask": plant((jax.random.randint(streams_of[8], (RELAY_SECTIONS, NQB, NKB), 0, 4) < 1).astype(jnp.int32), jax.random.fold_in(streams_of[8], 1), 0, 1),
        "span_offset": plant(jax.random.randint(streams_of[9], (RELAY_SECTIONS,), 0, 32768), jax.random.fold_in(streams_of[9], 1), 0, 32767).astype(jnp.int32),
    }


rope_base = 500000.0
neg_fill = -1e+30
norm_eps = 1e-05

def apply_rotation(values, token_positions):
    half = values.shape[-1] // 2
    freqs = rope_base ** (-2.0 * jnp.arange(half, dtype=jnp.float32) / values.shape[-1])
    angles = token_positions[:, None] * freqs[None, :]
    cosine = jnp.cos(angles)[:, None, :]
    sine = jnp.sin(angles)[:, None, :]
    first = values[..., :half]
    second = values[..., half:]
    return jnp.concatenate([first * cosine - second * sine, second * cosine + first * sine], axis=-1)

def one_layer(tokens, gain, w_query, key_projection, value_projection, w_out, key_cache, cached_value_rows, mask, offset):
    resid = tokens.astype(jnp.float32)
    mean_square = lax.optimization_barrier(jnp.mean(resid * resid, axis=-1, keepdims=True))
    input_normalized = (resid * lax.rsqrt(mean_square + norm_eps) * gain.astype(jnp.float32)).astype(jnp.bfloat16)
    token_positions = offset.astype(jnp.float32) + jnp.arange(SECTION_TOKENS, dtype=jnp.int32).astype(jnp.float32)
    query = jnp.dot(input_normalized, w_query, preferred_element_type=jnp.float32).reshape(SECTION_TOKENS, HQ, HEAD_SIZE)
    query = apply_rotation(query, token_positions).astype(jnp.bfloat16)
    key_unrotated = jnp.dot(input_normalized, key_projection, preferred_element_type=jnp.float32).astype(jnp.bfloat16)
    value_rows = jnp.dot(input_normalized, value_projection, preferred_element_type=jnp.float32).astype(jnp.bfloat16).reshape(SECTION_TOKENS, KEY_VALUE_HEADS, HEAD_SIZE)
    key = apply_rotation(key_unrotated.astype(jnp.float32).reshape(SECTION_TOKENS, KEY_VALUE_HEADS, HEAD_SIZE), token_positions).astype(jnp.bfloat16)
    visible = jnp.broadcast_to(mask[:, None, :, None] > 0, (NQB, QB, NKB, KB)).reshape(SECTION_TOKENS, CONTEXT_LENGTH)
    rows = jnp.arange(SECTION_TOKENS, dtype=jnp.int32)
    causal = rows[None, :] <= rows[:, None]
    scale = HEAD_SIZE ** (-0.5)

    def head_fn(item):
        query_head, head_id = item
        group_index = head_id // GROUP
        cache_keys = lax.dynamic_index_in_dim(key_cache, group_index, 1, keepdims=False)
        cache_values = lax.dynamic_index_in_dim(cached_value_rows, group_index, 1, keepdims=False)
        new_keys = lax.dynamic_index_in_dim(key, group_index, 1, keepdims=False)
        new_values = lax.dynamic_index_in_dim(value_rows, group_index, 1, keepdims=False)
        cache_scores = jnp.dot(query_head, cache_keys.T, preferred_element_type=jnp.float32) * scale
        self_scores = jnp.dot(query_head, new_keys.T, preferred_element_type=jnp.float32) * scale
        cache_scores = jnp.where(visible, cache_scores, neg_fill)
        self_scores = jnp.where(causal, self_scores, neg_fill)
        top = jnp.maximum(lax.optimization_barrier(jnp.max(cache_scores, axis=1)), lax.optimization_barrier(jnp.max(self_scores, axis=1)))
        cache_weights = jnp.where(visible, jnp.exp(cache_scores - top[:, None]), 0.0)
        self_weights = jnp.where(causal, jnp.exp(self_scores - top[:, None]), 0.0)
        total = lax.optimization_barrier(jnp.sum(cache_weights, axis=1)) + lax.optimization_barrier(jnp.sum(self_weights, axis=1))
        summed = jnp.dot(cache_weights.astype(jnp.bfloat16), cache_values, preferred_element_type=jnp.float32)
        summed = summed + jnp.dot(self_weights.astype(jnp.bfloat16), new_values, preferred_element_type=jnp.float32)
        return (summed / total[:, None]).astype(jnp.bfloat16)
    heads_out = lax.map(head_fn, (jnp.transpose(query, (1, 0, 2)), jnp.arange(HQ, dtype=jnp.int32)))
    attention = jnp.transpose(heads_out, (1, 0, 2)).reshape(SECTION_TOKENS, HQ * HEAD_SIZE)
    projected = jnp.dot(attention, w_out, preferred_element_type=jnp.float32)
    return (resid + projected).astype(jnp.bfloat16)

def reference(tokens, norm_gain, w_query, key_projection, value_projection, w_out, key_cache, cached_value_rows, cache_mask, span_offset):
    results = []
    for section_index in range(RELAY_SECTIONS):
        results.append(one_layer(tokens[section_index], norm_gain[section_index], w_query[section_index], key_projection[section_index], value_projection[section_index], w_out[section_index], key_cache[section_index], cached_value_rows[section_index], cache_mask[section_index], span_offset[section_index]))
    stacked = jnp.stack(results, axis=0)
    return jnp.roll(stacked, 1, axis=0)
```

```python
import functools

import jax
import jax.numpy as jnp
from jax import lax
from jax.experimental import pallas as pl
from jax.experimental.pallas import tpu as pltpu
from jax.sharding import PartitionSpec as P

MESH = pl.DeviceIdType.MESH
BF16 = jnp.bfloat16
F32 = jnp.float32
ROPE_BASE = 500000.0
NORM_EPS = 1e-05
NEG = -1e30
LOG2E = 1.4426950408889634
SCALE2 = 128 ** (-0.5) * LOG2E
VMEM_MAX = 64000 * 1024


def gray_inverse(v):
    return v ^ (v >> 1)


def natural_chip(b):
    return gray_inverse(b >> 2) * 4 + gray_inverse(b & 3)


def place():
    rank = lax.axis_index("seq")
    core = lax.rem(rank, 2)
    x = lax.rem(rank // 2, 4)
    y = rank // 8
    bits = (
        lax.rem(x + x // 2, 2),
        x // 2,
        lax.rem(y + y // 2, 2),
        y // 2,
    )

    def at(yy, xx, cc):
        return (yy * 4 + xx) * 2 + cc

    flip_x = x + 1 - 2 * lax.rem(x, 2)
    flip_y = y + 1 - 2 * lax.rem(y, 2)
    dims = (at(y, flip_x, core), at(y, 3 - x, core), at(flip_y, x, core), at(3 - y, x, core))
    partner = at(y, x, 1 - core)
    diagonal = at(y, flip_x, 1 - core)
    slot = 2 * lax.rem(x, 2) + core
    return core, bits, dims, partner, diagonal, slot


def region(bits, full, flipped=()):
    out = []
    for d in (3, 2, 1, 0):
        if d in full:
            out.append(slice(None))
        elif d in flipped:
            out.append(pl.ds(1 - bits[d], 1))
        else:
            out.append(pl.ds(bits[d], 1))
    return tuple(out)


def blocks(bits, full, flipped=()):
    free = [d for d in (3, 2, 1, 0) if d in full]
    out = []
    for i in range(1 << len(free)):
        index = {}
        for k, d in enumerate(free):
            index[d] = (i >> (len(free) - 1 - k)) & 1
        row = []
        for d in (3, 2, 1, 0):
            if d in index:
                row.append(index[d])
            elif d in flipped:
                row.append(1 - bits[d])
            else:
                row.append(bits[d])
        out.append(tuple(row))
    return out


def static_bits(b):
    return ((b >> 3) & 1, (b >> 2) & 1, (b >> 1) & 1, b & 1)


def greet(targets):
    barrier = pltpu.get_barrier_semaphore()
    for t in targets:
        pl.semaphore_signal(barrier, inc=1, device_id=t, device_id_type=MESH)
    pl.semaphore_wait(barrier, len(targets))


def push(src, dst, ssem, rsem, target):
    return pltpu.make_async_remote_copy(
        src_ref=src, dst_ref=dst, send_sem=ssem, recv_sem=rsem,
        device_id=target, device_id_type=MESH,
    )


def gather_torus(buf, core, bits, dims, partner, ssem, rsem, cssem, crsem, fillers):
    own = region(bits, ())
    crossing = []
    sent = []
    last = [None] * 4
    for p in range(4):
        c = push(buf.at[(core, p) + own], buf.at[(core, p) + own], cssem.at[p, 0], crsem.at[p, 0], {"seq": partner})
        crossing.append(c)
    done = [[] for _ in range(4)]
    for s in range(5):
        for p in range(4):
            if s > 0:
                d = (p + s - 1) % 4
                last[p].wait_recv()
                got = region(bits, done[p], (d,))
                c = push(buf.at[(core, p) + got], buf.at[(core, p) + got], cssem.at[p, s], crsem.at[p, s], {"seq": partner})
                c.start()
                crossing.append(c)
                done[p].append(d)
            if s < 4:
                d = (p + s) % 4
                have = region(bits, done[p])
                c = push(buf.at[(core, p) + have], buf.at[(core, p) + have], ssem.at[p, s], rsem.at[p, s], {"seq": dims[d]})
                c.start()
                sent.append(c)
                last[p] = c
        if s == 0:
            for c in crossing:
                c.start()
        if s < 4 and fillers[s] is not None:
            fillers[s]()
    return sent, crossing


def front_kernel(
    tok, gain, wq, kp, vp, cosf, sinf,
    q_out, self_o, self_l,
    nrm, prt, xbuf, wbuf, kbuf, vbuf, wkv, qbuf, kvbuf, kvn, qn, accq, acckv, qh,
    wsem, psem, ssem, rsem, cssem, crsem, ssem2, rsem2, cssem2, crsem2, kssem, krsem, osem,
):
    core, bits, dims, partner, diagonal, slot = place()
    loads = [
        pltpu.make_async_copy(wq, wbuf, wsem.at[0]),
        pltpu.make_async_copy(kp, kbuf, wsem.at[1]),
        pltpu.make_async_copy(vp, vbuf, wsem.at[2]),
    ]
    for c in loads:
        c.start()
    greet([{"seq": t} for t in (partner, diagonal) + dims])
    xf = tok[...].astype(F32)
    ms = jnp.mean(xf * xf, axis=-1, keepdims=True)
    xn = (xf * lax.rsqrt(ms + NORM_EPS) * gain[...].astype(F32)).astype(BF16)
    nrm[0] = xn[:, :4096]
    nrm[1] = xn[:, 4096:]
    swap = push(nrm.at[1 - core], prt, psem.at[0], psem.at[1], {"seq": partner})
    swap.start()
    swap.wait()
    mine = nrm[core].astype(F32)
    other = prt[...].astype(F32)
    pair = jnp.concatenate(
        [jnp.where(core == 0, mine, other), jnp.where(core == 0, other, mine)], axis=0
    ).astype(BF16)
    for p in range(4):
        xbuf[core, p, bits[3], bits[2], bits[1], bits[0]] = pair[:, 1024 * p : 1024 * (p + 1)]

    def join_kv():
        loads[1].wait()
        loads[2].wait()

        @pl.loop(0, 16)
        def _(i):
            r = pl.ds(pl.multiple_of(i * 512, 512), 512)
            wkv[r, :] = jnp.concatenate([kbuf[r, :], vbuf[r, :]], axis=1)

    def clear():
        accq[...] = jnp.zeros_like(accq)
        acckv[...] = jnp.zeros_like(acckv)

    sent, crossing = gather_torus(
        xbuf, core, bits, dims, partner, ssem, rsem, cssem, crsem, [None, clear, join_kv, None]
    )
    loads[0].wait()

    def multiply(half):
        @pl.loop(0, 4)
        def _(p):
            xb = xbuf[half, p].reshape(256, 1024)
            r = pl.ds(pl.multiple_of(half * 4096 + p * 1024, 1024), 1024)
            accq[...] += jnp.dot(xb, wbuf[r, :], preferred_element_type=F32)
            acckv[...] += jnp.dot(xb, wkv[r, :], preferred_element_type=F32)

    multiply(core)
    for c in crossing:
        c.wait_recv()
    multiply(1 - core)
    for b in range(16):
        n = natural_chip(b)
        qn[16 * n : 16 * n + 16, :] = accq[16 * b : 16 * b + 16, :]
        kvn[16 * n : 16 * n + 16, :] = acckv[16 * b : 16 * b + 16, :]
    kvbuf[slot] = kvn[...].astype(BF16)
    near = []
    for k, t in enumerate((partner, dims[0], diagonal)):
        c = push(kvbuf.at[slot], kvbuf.at[slot], kssem.at[k], krsem.at[k], {"seq": t})
        c.start()
        near.append(c)

    def rotate(u):
        return (u * cosf[...] + pltpu.roll(u, 64, 1) * sinf[...]).astype(BF16)

    for j in range(2):
        r = rotate(qn[:, 128 * j : 128 * (j + 1)])
        qh[j] = r
        for u in range(2):
            qbuf[core, 2 * j + u, bits[3], bits[2], bits[1], bits[0]] = r[128 * u : 128 * (u + 1)]

    def self_part():
        for c in near:
            c.wait_recv()
        key = rotate(jnp.concatenate([kvbuf[m][:, :32] for m in range(4)], axis=1).astype(F32))
        val = jnp.concatenate([kvbuf[m][:, 32:64] for m in range(4)], axis=1)
        seen = lax.broadcasted_iota(jnp.int32, (256, 256), 1) <= lax.broadcasted_iota(jnp.int32, (256, 256), 0)
        for j in range(2):
            sc = lax.dot_general(qh[j], key, (((1,), (1,)), ((), ())), preferred_element_type=F32)
            sc = jnp.where(seen, sc * SCALE2, NEG)
            top = jnp.max(sc, axis=1, keepdims=True)
            w = jnp.where(seen, jnp.exp2(sc - top), 0.0)
            total = jnp.sum(w, axis=1, keepdims=True)
            out = jnp.dot(w.astype(BF16), val, preferred_element_type=F32)
            self_o[j] = out / total
            self_l[j] = jnp.broadcast_to(top + jnp.log2(total), (256, 128))

    sent2, crossing2 = gather_torus(
        qbuf, core, bits, dims, partner, ssem2, rsem2, cssem2, crsem2, [None, self_part, None, None]
    )
    outs = []
    for p in range(4):
        c = pltpu.make_async_copy(qbuf.at[core, p], q_out.at[core, p], osem.at[0, p])
        c.start()
        outs.append(c)
    for c in crossing2:
        c.wait_recv()
    for p in range(4):
        c = pltpu.make_async_copy(qbuf.at[1 - core, p], q_out.at[1 - core, p], osem.at[1, p])
        c.start()
        outs.append(c)
    for c in sent + crossing + sent2 + crossing2 + near:
        c.wait_send()
    for c in outs:
        c.wait()


def front(tokens, gain, wq, kp, vp, cosf, sinf):
    any_spec = pl.BlockSpec(memory_space=pl.ANY)
    vmem = pl.BlockSpec(memory_space=pltpu.VMEM)
    dma = pltpu.SemaphoreType.DMA
    return pl.pallas_call(
        front_kernel,
        out_shape=(
            jax.ShapeDtypeStruct((2, 4, 2, 2, 2, 2, 128, 128), BF16),
            jax.ShapeDtypeStruct((2, 256, 128), F32),
            jax.ShapeDtypeStruct((2, 256, 128), F32),
        ),
        in_specs=[vmem, vmem, any_spec, any_spec, any_spec, vmem, vmem],
        out_specs=(any_spec, vmem, vmem),
        scratch_shapes=[
            pltpu.VMEM((2, 8, 4096), BF16),
            pltpu.VMEM((8, 4096), BF16),
            pltpu.VMEM((2, 4, 2, 2, 2, 2, 16, 1024), BF16),
            pltpu.VMEM((8192, 256), BF16),
            pltpu.VMEM((8192, 32), BF16),
            pltpu.VMEM((8192, 32), BF16),
            pltpu.VMEM((8192, 64), BF16),
            pltpu.VMEM((2, 4, 2, 2, 2, 2, 128, 128), BF16),
            pltpu.VMEM((4, 256, 64), BF16),
            pltpu.VMEM((256, 64), F32),
            pltpu.VMEM((256, 256), F32),
            pltpu.VMEM((256, 256), F32),
            pltpu.VMEM((256, 64), F32),
            pltpu.VMEM((2, 256, 128), BF16),
            dma((3,)), dma((2,)),
            dma((4, 4)), dma((4, 4)), dma((4, 5)), dma((4, 5)),
            dma((4, 4)), dma((4, 4)), dma((4, 5)), dma((4, 5)),
            dma((3,)), dma((3,)), dma((2, 4)),
        ],
        compiler_params=pltpu.CompilerParams(
            collective_id=0, has_side_effects=True, vmem_limit_bytes=VMEM_MAX
        ),
        name="front",
    )(tokens, gain, wq, kp, vp, cosf, sinf)


NG = 2


def cache_kernel(
    mask, q_hbm, k_hbm, v_hbm, o_hbm, lse,
    q, kraw, vraw, kt, vt, sbuf, mx, ls, acc, obuf, listed, count,
    qsem, ksem, vsem, osem,
):
    qcopy = pltpu.make_async_copy(q_hbm, q, qsem.at[0])
    chunk = 256
    loads = []
    for i in range(8):
        r = pl.ds(i * chunk, chunk)
        kc = pltpu.make_async_copy(k_hbm.at[r], kraw.at[r], ksem.at[i])
        vc = pltpu.make_async_copy(v_hbm.at[r], vraw.at[r], vsem.at[i])
        kc.start()
        vc.start()
        loads.append((kc, vc))
    qcopy.start()
    lse[...] = jnp.zeros_like(lse)

    @pl.loop(0, 8)
    def _(b):
        def put(k, n):
            listed[b, n] = k
            return n + jnp.where(mask[b, k] > 0, 1, 0)

        count[b] = lax.fori_loop(0, 16, put, 0)

    for i in range(8):
        for c, raw, out in ((loads[i][0], kraw, kt), (loads[i][1], vraw, vt)):
            c.wait()

            @pl.loop(0, chunk // 64)
            def _(t):
                r = pl.ds(pl.multiple_of(i * chunk + t * 64, 64), 64)
                out[:, r, :] = jnp.swapaxes(raw[r], 0, 1)

    qcopy.wait()
    lane = lax.broadcasted_iota(jnp.int32, (32, 128), 1)

    @pl.loop(0, 8 // NG)
    def _(gp):
        gammas = []
        for e in range(NG):
            gamma = gp * NG + e
            yb = gamma // 2
            gammas.append((gamma, 2 * (yb ^ (yb >> 1)) + lax.rem(gamma, 2)))

        @pl.loop(0, 8)
        def _(b):
            u = b // 4
            rows = pl.ds(pl.multiple_of(lax.rem(b, 4) * 32, 32), 32)
            n = count[b]
            pairs = n // 2
            qs = []
            for e, (gamma, g) in enumerate(gammas):
                qs.append(q[:, :, u, pl.ds(2 * gamma, 2), rows, :].reshape(256, 128))
                mx[e] = jnp.full((256, 128), NEG, F32)
                ls[e] = jnp.zeros((256, 128), F32)
                acc[e] = jnp.zeros((256, 128), F32)

            def at(k):
                return pl.ds(pl.multiple_of(listed[b, k] * 128, 128), 128)

            @pl.loop(0, pairs)
            def _(i):
                r0, r1 = at(2 * i), at(2 * i + 1)
                for e, (gamma, g) in enumerate(gammas):
                    kk = jnp.concatenate([kt[g, r0, :], kt[g, r1, :]], axis=0)
                    sc = lax.dot_general(qs[e], kk, (((1,), (1,)), ((), ())), preferred_element_type=F32)
                    sbuf[e, i] = sc
                    mx[e] = jnp.maximum(mx[e], jnp.maximum(sc[:, :128], sc[:, 128:]))

            @pl.when(lax.rem(n, 2) == 1)
            def _():
                r0 = at(n - 1)
                for e, (gamma, g) in enumerate(gammas):
                    sc = lax.dot_general(qs[e], kt[g, r0, :], (((1,), (1,)), ((), ())), preferred_element_type=F32)
                    sbuf[e, pairs, :, 0:128] = sc
                    mx[e] = jnp.maximum(mx[e], sc)

            tops = [jnp.max(mx[e], axis=1, keepdims=True) * SCALE2 for e in range(NG)]

            @pl.loop(0, pairs)
            def _(i):
                r0, r1 = at(2 * i), at(2 * i + 1)
                for e, (gamma, g) in enumerate(gammas):
                    w = jnp.exp2(sbuf[e, i] * SCALE2 - tops[e])
                    ls[e] += w[:, :128] + w[:, 128:]
                    vv = jnp.concatenate([vt[g, r0, :], vt[g, r1, :]], axis=0)
                    acc[e] += jnp.dot(w.astype(BF16), vv, preferred_element_type=F32)

            @pl.when(lax.rem(n, 2) == 1)
            def _():
                r0 = at(n - 1)
                for e, (gamma, g) in enumerate(gammas):
                    w = jnp.exp2(sbuf[e, pairs, :, 0:128] * SCALE2 - tops[e])
                    ls[e] += w
                    acc[e] += jnp.dot(w.astype(BF16), vt[g, r0, :], preferred_element_type=F32)

            for e, (gamma, g) in enumerate(gammas):
                total = jnp.sum(ls[e], axis=1, keepdims=True)
                safe = jnp.where(total > 0.0, total, 1.0)
                out = (acc[e] / safe).astype(BF16)
                obuf[:, :, u, pl.ds(2 * gamma, 2), rows, :] = out.reshape(2, 2, 2, 32, 128)
                level = jnp.where(total > 0.0, tops[e] + jnp.log2(safe), NEG)
                for m in range(8):
                    cc, j, ee = m // 4, (m // 2) % 2, m % 2
                    old = lse[cc, j, u, rows, :]
                    lse[cc, j, u, rows, :] = jnp.where(
                        lane == 2 * gamma + ee, level[32 * m : 32 * (m + 1)], old
                    )

    outs = []
    for cc in range(2):
        c = pltpu.make_async_copy(obuf.at[cc], o_hbm.at[cc], osem.at[cc])
        c.start()
        outs.append(c)
    for c in outs:
        c.wait()


def cache_attention(mask, q, k, v):
    any_spec = pl.BlockSpec(memory_space=pl.ANY)
    vmem = pl.BlockSpec(memory_space=pltpu.VMEM)
    dma = pltpu.SemaphoreType.DMA
    shape = (2, 2, 2, 16, 128, 128)
    return pl.pallas_call(
        cache_kernel,
        out_shape=(
            jax.ShapeDtypeStruct(shape, BF16),
            jax.ShapeDtypeStruct((2, 2, 2, 128, 128), F32),
        ),
        in_specs=[pl.BlockSpec(memory_space=pltpu.SMEM), any_spec, any_spec, any_spec],
        out_specs=(any_spec, vmem),
        scratch_shapes=[
            pltpu.VMEM(shape, BF16),
            pltpu.VMEM((2048, 8, 128), BF16),
            pltpu.VMEM((2048, 8, 128), BF16),
            pltpu.VMEM((8, 2048, 128), BF16),
            pltpu.VMEM((8, 2048, 128), BF16),
            pltpu.VMEM((NG, 8, 256, 256), F32),
            pltpu.VMEM((NG, 256, 128), F32),
            pltpu.VMEM((NG, 256, 128), F32),
            pltpu.VMEM((NG, 256, 128), F32),
            pltpu.VMEM(shape, BF16),
            pltpu.SMEM((8, 17), jnp.int32),
            pltpu.SMEM((8,), jnp.int32),
            dma((1,)), dma((8,)), dma((8,)), dma((2,)),
        ],
        compiler_params=pltpu.CompilerParams(vmem_limit_bytes=VMEM_MAX),
        name="cache",
    )(mask, q, k, v)


def blend(a, b):
    wa = 1.0 / (1.0 + jnp.exp2(b - a))
    wb = 1.0 / (1.0 + jnp.exp2(a - b))
    level = jnp.maximum(a, b) + jnp.log2(1.0 + jnp.exp2(-jnp.abs(a - b)))
    return wa, wb, level


def columns(rows):
    stacked = jnp.concatenate(rows, axis=0) if len(rows) > 1 else rows[0]
    fill = jnp.zeros((128 - len(rows), 128), F32)
    return jnp.concatenate([stacked, fill], axis=0).T


def back_kernel(
    o_hbm, lse, self_o, self_l, w_out, tok, out,
    ob, oc, lsec, acc, lrow, snd0, snd1, snd2, snd3, rcv0, rcv1, rcv2, rcv3,
    rl0, rl1, rl2, rl3, sl0, sl1, sl2, sl3, att, wbuf, ysend, yrecv, yacc, tokp, res, hout,
    ys0, ys1, ys2, ys3, yr0, yr1, yr2, yr3,
    wsem, obsem, ocs, ocr, lss, lsr, tsem, ss, rs, ls_, lr_, ycs, ycr, yss, yrs, hss, hrs,
):
    core, bits, dims, partner, _, _ = place()
    section = lax.axis_index("section")
    rank = lax.axis_index("seq")
    chip = rank // 2
    up = lax.rem(section + 1, 4)
    down = lax.rem(section + 3, 4)
    load_w = pltpu.make_async_copy(w_out, wbuf, wsem.at[0])
    own_loads = []
    for p in range(4):
        c = pltpu.make_async_copy(o_hbm.at[core, p], ob.at[p], obsem.at[p])
        c.start()
        own_loads.append(c)
    load_w.start()
    targets = [{"seq": t} for t in (partner,) + dims]
    for sec in (up, down):
        for cc in range(2):
            targets.append({"section": sec, "seq": chip * 2 + cc})
    greet(targets)
    waits = []
    lcopy = push(lse.at[1 - core], lsec, lss.at[0], lsr.at[0], {"seq": partner})
    lcopy.start()
    ocopies = []
    for p in range(4):
        c = push(o_hbm.at[1 - core, p], oc.at[p], ocs.at[p], ocr.at[p], {"seq": partner})
        c.start()
        ocopies.append(c)
    tcopy = push(
        tok.at[:, pl.ds(pl.multiple_of((1 - core) * 4096, 4096), 4096)], tokp, tsem.at[0], tsem.at[1], {"seq": partner}
    )
    tcopy.start()
    waits += ocopies + [lcopy, tcopy]

    snd = (snd0, snd1, snd2, snd3)
    rcv = (rcv0, rcv1, rcv2, rcv3)
    rl = (rl0, rl1, rl2, rl3)
    sl = (sl0, sl1, sl2, sl3)
    lcopy.wait_recv()
    done = [[] for _ in range(4)]
    flight = [None] * 4

    def remaining(p):
        return [d for d in range(4) if d not in done[p]]

    def start_step(p, s):
        d = (p + s) % 4
        rest = [k for k in remaining(p) if k != d]
        for i, idx in enumerate(blocks(bits, rest, (d,))):
            snd[s][p, i] = acc[(p,) + idx].astype(BF16)
            sl[s][p, i] = lrow[(p,) + idx]
        c1 = push(snd[s].at[p], rcv[s].at[p], ss.at[p, s], rs.at[p, s], {"seq": dims[d]})
        c2 = push(sl[s].at[p], rl[s].at[p], ls_.at[p, s], lr_.at[p, s], {"seq": dims[d]})
        c2.start()
        c1.start()
        done[p].append(d)
        flight[p] = (c1, c2)
        waits.extend((c1, c2))

    for s in range(5):
        for p in range(4):
            if s == 0:
                own_loads[p].wait()
                ocopies[p].wait_recv()
                wa, wb, level = blend(lse[core, p], lsec[p])
                turned = level.T
                for b in range(16):
                    sb = static_bits(b)
                    acc[(p,) + sb] = (
                        ob[(p,) + sb].astype(F32) * wa[:, b : b + 1]
                        + oc[(p,) + sb].astype(F32) * wb[:, b : b + 1]
                    )
                    lrow[(p,) + sb] = turned[b : b + 1, :]
            else:
                c1, c2 = flight[p]
                c2.wait_recv()
                c1.wait_recv()
                keep = blocks(bits, remaining(p))
                n = len(keep)
                got = rl[s - 1][p].reshape(n, 1, 128)
                a_rows = [lrow[(p,) + idx] for idx in keep]
                wa_rows, wb_rows = [], []
                for i, idx in enumerate(keep):
                    wa, wb, level = blend(a_rows[i], got[i])
                    wa_rows.append(wa)
                    wb_rows.append(wb)
                    lrow[(p,) + idx] = level
                wac, wbc = columns(wa_rows), columns(wb_rows)
                for i, idx in enumerate(keep):
                    acc[(p,) + idx] = (
                        acc[(p,) + idx] * wac[:, i : i + 1]
                        + rcv[s - 1][p, i].astype(F32) * wbc[:, i : i + 1]
                    )
            if s < 4:
                start_step(p, s)

    me = (bits[3], bits[2], bits[1], bits[0])
    for p in range(4):
        j, u = p // 2, p % 2
        level = jnp.broadcast_to(lrow[(p,) + me], (128, 128)).T
        mine = self_l[j, 128 * u : 128 * (u + 1), :]
        wa, wb, _ = blend(level, mine)
        merged = acc[(p,) + me] * wa + self_o[j, 128 * u : 128 * (u + 1), :] * wb
        att[128 * u : 128 * (u + 1), 128 * j : 128 * (j + 1)] = merged.astype(BF16)
    load_w.wait()

    def cols(half, p):
        return pl.ds(pl.multiple_of(half * 4096 + p * 1024, 1024), 1024)

    @pl.loop(0, 4)
    def _(p):
        r = jnp.dot(att[...], wbuf[:, cols(1 - core, p)], preferred_element_type=F32).astype(BF16)
        for b in range(16):
            n = natural_chip(b)
            ysend[(p,) + static_bits(b)] = r[16 * n : 16 * n + 16, :]
        push(ysend.at[p], yrecv.at[p], ycs.at[p], ycr.at[p], {"seq": partner}).start()

    @pl.loop(0, 4)
    def _(p):
        r = jnp.dot(att[...], wbuf[:, cols(core, p)], preferred_element_type=F32)
        for b in range(16):
            n = natural_chip(b)
            yacc[(p,) + static_bits(b)] = r[16 * n : 16 * n + 16, :]

    ys = (ys0, ys1, ys2, ys3)
    yr = (yr0, yr1, yr2, yr3)
    done = [[] for _ in range(4)]
    for s in range(5):
        for p in range(4):
            if s == 0:
                c = push(ysend.at[p], yrecv.at[p], ycs.at[p], ycr.at[p], {"seq": partner})
                waits.append(c)
                c.wait_recv()
                for b in range(16):
                    sb = static_bits(b)
                    yacc[(p,) + sb] += yrecv[(p,) + sb].astype(F32)
            else:
                flight[p].wait_recv()
                for i, idx in enumerate(blocks(bits, remaining(p))):
                    yacc[(p,) + idx] += yr[s - 1][p, i].astype(F32)
            if s < 4:
                d = (p + s) % 4
                rest = [k for k in remaining(p) if k != d]
                for i, idx in enumerate(blocks(bits, rest, (d,))):
                    ys[s][p, i] = yacc[(p,) + idx].astype(BF16)
                c = push(ys[s].at[p], yr[s].at[p], yss.at[p, s], yrs.at[p, s], {"seq": dims[d]})
                c.start()
                done[p].append(d)
                flight[p] = c
                waits.append(c)

    tcopy.wait_recv()
    mine = tok[:, pl.ds(pl.multiple_of(core * 4096, 4096), 4096)].astype(F32)
    other = tokp[...].astype(F32)
    low = jnp.where(core == 0, mine, other)
    high = jnp.where(core == 0, other, mine)
    for p in range(4):
        total = yacc[(p,) + me]
        span = slice(1024 * p, 1024 * (p + 1))
        res[0, :, span] = (low[:, span] + total[0:8]).astype(BF16)
        res[1, :, span] = (high[:, span] + total[8:16]).astype(BF16)
    final = []
    for cc in range(2):
        c = push(
            res.at[cc], hout.at[core], hss.at[cc], hrs.at[core], {"section": up, "seq": chip * 2 + cc},
        )
        c.start()
        waits.append(c)
    for cc in range(2):
        push(
            res.at[cc], hout.at[cc], hss.at[cc], hrs.at[cc], {"section": up, "seq": chip * 2 + cc},
        ).wait_recv()
        out[:, 4096 * cc : 4096 * (cc + 1)] = hout[cc]
    for c in waits:
        c.wait_send()


def back(o, lse, self_o, self_l, w_out, tokens):
    any_spec = pl.BlockSpec(memory_space=pl.ANY)
    vmem = pl.BlockSpec(memory_space=pltpu.VMEM)
    dma = pltpu.SemaphoreType.DMA
    bit = (2, 2, 2, 2)
    steps = (8, 4, 2, 1)
    scratch = [
        pltpu.VMEM((4,) + bit + (128, 128), BF16),
        pltpu.VMEM((4,) + bit + (128, 128), BF16),
        pltpu.VMEM((4, 128, 128), F32),
        pltpu.VMEM((4,) + bit + (128, 128), F32),
        pltpu.VMEM((4,) + bit + (1, 128), F32),
    ]
    scratch += [pltpu.VMEM((4, n, 128, 128), BF16) for n in steps]
    scratch += [pltpu.VMEM((4, n, 128, 128), BF16) for n in steps]
    scratch += [pltpu.VMEM((4, n, 1, 128), F32) for n in steps + steps]
    scratch += [
        pltpu.VMEM((256, 256), BF16),
        pltpu.VMEM((256, 8192), BF16),
        pltpu.VMEM((4,) + bit + (16, 1024), BF16),
        pltpu.VMEM((4,) + bit + (16, 1024), BF16),
        pltpu.VMEM((4,) + bit + (16, 1024), F32),
        pltpu.VMEM((8, 4096), BF16),
        pltpu.VMEM((2, 8, 4096), BF16),
        pltpu.VMEM((2, 8, 4096), BF16),
    ]
    scratch += [pltpu.VMEM((4, n, 16, 1024), BF16) for n in steps]
    scratch += [pltpu.VMEM((4, n, 16, 1024), BF16) for n in steps]
    scratch += [
        dma((1,)), dma((4,)), dma((4,)), dma((4,)), dma((1,)), dma((1,)), dma((2,)),
        dma((4, 4)), dma((4, 4)), dma((4, 4)), dma((4, 4)),
        dma((4,)), dma((4,)), dma((4, 4)), dma((4, 4)), dma((2,)), dma((2,)),
    ]
    return pl.pallas_call(
        back_kernel,
        out_shape=jax.ShapeDtypeStruct((8, 8192), BF16),
        in_specs=[any_spec, vmem, vmem, vmem, any_spec, vmem],
        out_specs=vmem,
        scratch_shapes=scratch,
        compiler_params=pltpu.CompilerParams(
            collective_id=1, has_side_effects=True, vmem_limit_bytes=VMEM_MAX
        ),
        name="back",
    )(o, lse, self_o, self_l, w_out, tokens)


def on_device(
    tokens, norm_gain, w_query, key_projection, value_projection, w_out,
    key_cache, cached_value_rows, cache_mask, span_offset,
):
    offset = span_offset[0].astype(F32)
    positions = offset + jnp.arange(256, dtype=jnp.int32).astype(F32)
    freqs = ROPE_BASE ** (-2.0 * jnp.arange(64, dtype=F32) / 128)
    angles = positions[:, None] * freqs[None, :]
    cosine, sine = jnp.cos(angles), jnp.sin(angles)
    cosf = jnp.concatenate([cosine, cosine], axis=1)
    sinf = jnp.concatenate([-sine, sine], axis=1)
    q, self_o, self_l = front(
        tokens[0], norm_gain, w_query[0], key_projection[0], value_projection[0], cosf, sinf
    )
    o, lse = cache_attention(
        cache_mask[0], q.reshape(2, 2, 2, 16, 128, 128), key_cache[0], cached_value_rows[0]
    )
    bit = (2, 2, 2, 2)
    handed = back(
        o.reshape((2, 4) + bit + (128, 128)), lse.reshape(2, 4, 128, 128), self_o, self_l, w_out[0], tokens[0]
    )
    return handed[None]


def solution(mesh):
    placed = (
        P("section", "seq", None),
        P("section", None),
        P("section", None, "seq"),
        P("section", None, "seq"),
        P("section", None, "seq"),
        P("section", "seq", None),
        P("section", "seq", None, None),
        P("section", "seq", None, None),
        P("section", None, "seq"),
        P("section"),
    )
    return jax.shard_map(
        on_device, mesh=mesh, in_specs=placed, out_specs=P("section", "seq", None), check_vma=False
    )
```

```python
import functools

import jax
import jax.numpy as jnp
from jax import lax
from jax.experimental import pallas as pl
from jax.experimental.pallas import tpu as pltpu
from jax.sharding import PartitionSpec as P

MESH = pl.DeviceIdType.MESH
BF16 = jnp.bfloat16
F32 = jnp.float32
ROPE_BASE = 500000.0
NORM_EPS = 1e-05
NEG = -1e30
LOG2E = 1.4426950408889634
SCALE2 = 128 ** (-0.5) * LOG2E
VMEM_MAX = 64000 * 1024


def gray_inverse(v):
    return v ^ (v >> 1)


def natural_chip(b):
    return gray_inverse(b >> 2) * 4 + gray_inverse(b & 3)


def place():
    rank = lax.axis_index("seq")
    core = lax.rem(rank, 2)
    x = lax.rem(rank // 2, 4)
    y = rank // 8
    bits = (
        lax.rem(x + x // 2, 2),
        x // 2,
        lax.rem(y + y // 2, 2),
        y // 2,
    )

    def at(yy, xx, cc):
        return (yy * 4 + xx) * 2 + cc

    flip_x = x + 1 - 2 * lax.rem(x, 2)
    flip_y = y + 1 - 2 * lax.rem(y, 2)
    dims = (at(y, flip_x, core), at(y, 3 - x, core), at(flip_y, x, core), at(3 - y, x, core))
    partner = at(y, x, 1 - core)
    diagonal = at(y, flip_x, 1 - core)
    slot = 2 * lax.rem(x, 2) + core
    return core, bits, dims, partner, diagonal, slot


def region(bits, full, flipped=()):
    out = []
    for d in (3, 2, 1, 0):
        if d in full:
            out.append(slice(None))
        elif d in flipped:
            out.append(pl.ds(1 - bits[d], 1))
        else:
            out.append(pl.ds(bits[d], 1))
    return tuple(out)


def blocks(bits, full, flipped=()):
    free = [d for d in (3, 2, 1, 0) if d in full]
    out = []
    for i in range(1 << len(free)):
        index = {}
        for k, d in enumerate(free):
            index[d] = (i >> (len(free) - 1 - k)) & 1
        row = []
        for d in (3, 2, 1, 0):
            if d in index:
                row.append(index[d])
            elif d in flipped:
                row.append(1 - bits[d])
            else:
                row.append(bits[d])
        out.append(tuple(row))
    return out


def static_bits(b):
    return ((b >> 3) & 1, (b >> 2) & 1, (b >> 1) & 1, b & 1)


def greet(targets):
    barrier = pltpu.get_barrier_semaphore()
    for t in targets:
        pl.semaphore_signal(barrier, inc=1, device_id=t, device_id_type=MESH)
    pl.semaphore_wait(barrier, len(targets))


def push(src, dst, ssem, rsem, target):
    return pltpu.make_async_remote_copy(
        src_ref=src, dst_ref=dst, send_sem=ssem, recv_sem=rsem,
        device_id=target, device_id_type=MESH,
    )


def gather_torus(buf, core, bits, dims, partner, ssem, rsem, cssem, crsem, fillers):
    own = region(bits, ())
    crossing = []
    sent = []
    last = [None] * 4
    for p in range(4):
        c = push(buf.at[(core, p) + own], buf.at[(core, p) + own], cssem.at[p, 0], crsem.at[p, 0], {"seq": partner})
        crossing.append(c)
    done = [[] for _ in range(4)]
    for s in range(5):
        for p in range(4):
            if s > 0:
                d = (p + s - 1) % 4
                last[p].wait_recv()
                got = region(bits, done[p], (d,))
                c = push(buf.at[(core, p) + got], buf.at[(core, p) + got], cssem.at[p, s], crsem.at[p, s], {"seq": partner})
                c.start()
                crossing.append(c)
                done[p].append(d)
            if s < 4:
                d = (p + s) % 4
                have = region(bits, done[p])
                c = push(buf.at[(core, p) + have], buf.at[(core, p) + have], ssem.at[p, s], rsem.at[p, s], {"seq": dims[d]})
                c.start()
                sent.append(c)
                last[p] = c
        if s == 0:
            for c in crossing:
                c.start()
        if s < 4 and fillers[s] is not None:
            fillers[s]()
    return sent, crossing


def front_kernel(
    tok, gain, wq, kp, vp, cosf, sinf,
    q_out, self_o, self_l,
    nrm, prt, xbuf, wbuf, wkv, qbuf, kvbuf, kvn, qn, accq, acckv, qh,
    wsem, psem, ssem, rsem, cssem, crsem, ssem2, rsem2, cssem2, crsem2, kssem, krsem, osem,
):
    core, bits, dims, partner, diagonal, slot = place()
    loads = [
        pltpu.make_async_copy(wq, wbuf, wsem.at[0]),
        pltpu.make_async_copy(kp, wkv.at[0:32], wsem.at[1]),
        pltpu.make_async_copy(vp, wkv.at[32:64], wsem.at[2]),
    ]
    for c in loads:
        c.start()
    greet([{"seq": t} for t in (partner, diagonal) + dims])
    xf = tok[...].astype(F32)
    ms = jnp.mean(xf * xf, axis=-1, keepdims=True)
    xn = (xf * lax.rsqrt(ms + NORM_EPS) * gain[...].astype(F32)).astype(BF16)
    nrm[0] = xn[:, :4096]
    nrm[1] = xn[:, 4096:]
    swap = push(nrm.at[1 - core], prt, psem.at[0], psem.at[1], {"seq": partner})
    swap.start()
    swap.wait()
    mine = nrm[core].astype(F32)
    other = prt[...].astype(F32)
    pair = jnp.concatenate(
        [jnp.where(core == 0, mine, other), jnp.where(core == 0, other, mine)], axis=0
    ).astype(BF16)
    for p in range(4):
        xbuf[core, p, bits[3], bits[2], bits[1], bits[0]] = pair[:, 1024 * p : 1024 * (p + 1)]

    def clear():
        accq[...] = jnp.zeros_like(accq)
        acckv[...] = jnp.zeros_like(acckv)

    sent, crossing = gather_torus(
        xbuf, core, bits, dims, partner, ssem, rsem, cssem, crsem, [None, clear, None, None]
    )
    for c in loads:
        c.wait()

    def multiply(half):
        @pl.loop(0, 4)
        def _(p):
            xb = xbuf[half, p].reshape(256, 1024)
            r = pl.ds(pl.multiple_of(half * 4096 + p * 1024, 1024), 1024)
            accq[...] += jnp.dot(xb, wbuf[r, :], preferred_element_type=F32)
            acckv[...] += lax.dot_general(
                xb, wkv[:, r], (((1,), (1,)), ((), ())), preferred_element_type=F32
            )

    multiply(core)
    for c in crossing:
        c.wait_recv()
    multiply(1 - core)
    for b in range(16):
        n = natural_chip(b)
        qn[16 * n : 16 * n + 16, :] = accq[16 * b : 16 * b + 16, :]
        kvn[16 * n : 16 * n + 16, :] = acckv[16 * b : 16 * b + 16, :]
    kvbuf[slot] = kvn[...].astype(BF16)
    near = []
    for k, t in enumerate((partner, dims[0], diagonal)):
        c = push(kvbuf.at[slot], kvbuf.at[slot], kssem.at[k], krsem.at[k], {"seq": t})
        c.start()
        near.append(c)

    def rotate(u):
        return (u * cosf[...] + pltpu.roll(u, 64, 1) * sinf[...]).astype(BF16)

    for j in range(2):
        r = rotate(qn[:, 128 * j : 128 * (j + 1)])
        qh[j] = r
        for u in range(2):
            qbuf[core, 2 * j + u, bits[3], bits[2], bits[1], bits[0]] = r[128 * u : 128 * (u + 1)]

    def self_part():
        for c in near:
            c.wait_recv()
        key = rotate(jnp.concatenate([kvbuf[m][:, :32] for m in range(4)], axis=1).astype(F32))
        val = jnp.concatenate([kvbuf[m][:, 32:64] for m in range(4)], axis=1)
        seen = lax.broadcasted_iota(jnp.int32, (256, 256), 1) <= lax.broadcasted_iota(jnp.int32, (256, 256), 0)
        for j in range(2):
            sc = lax.dot_general(qh[j], key, (((1,), (1,)), ((), ())), preferred_element_type=F32)
            sc = jnp.where(seen, sc * SCALE2, NEG)
            top = jnp.max(sc, axis=1, keepdims=True)
            w = jnp.where(seen, jnp.exp2(sc - top), 0.0)
            total = jnp.sum(w, axis=1, keepdims=True)
            out = jnp.dot(w.astype(BF16), val, preferred_element_type=F32)
            self_o[j] = out / total
            self_l[j] = jnp.broadcast_to(top + jnp.log2(total), (256, 128))

    sent2, crossing2 = gather_torus(
        qbuf, core, bits, dims, partner, ssem2, rsem2, cssem2, crsem2, [None, self_part, None, None]
    )
    outs = []
    for p in range(4):
        c = pltpu.make_async_copy(qbuf.at[core, p], q_out.at[core, p], osem.at[0, p])
        c.start()
        outs.append(c)
    for c in crossing2:
        c.wait_recv()
    for p in range(4):
        c = pltpu.make_async_copy(qbuf.at[1 - core, p], q_out.at[1 - core, p], osem.at[1, p])
        c.start()
        outs.append(c)
    for c in sent + crossing + sent2 + crossing2 + near:
        c.wait_send()
    for c in outs:
        c.wait()


def front(tokens, gain, wq, kp, vp, cosf, sinf):
    any_spec = pl.BlockSpec(memory_space=pl.ANY)
    vmem = pl.BlockSpec(memory_space=pltpu.VMEM)
    dma = pltpu.SemaphoreType.DMA
    return pl.pallas_call(
        front_kernel,
        out_shape=(
            jax.ShapeDtypeStruct((2, 4, 2, 2, 2, 2, 128, 128), BF16),
            jax.ShapeDtypeStruct((2, 256, 128), F32),
            jax.ShapeDtypeStruct((2, 256, 128), F32),
        ),
        in_specs=[vmem, vmem, any_spec, any_spec, any_spec, vmem, vmem],
        out_specs=(any_spec, vmem, vmem),
        scratch_shapes=[
            pltpu.VMEM((2, 8, 4096), BF16),
            pltpu.VMEM((8, 4096), BF16),
            pltpu.VMEM((2, 4, 2, 2, 2, 2, 16, 1024), BF16),
            pltpu.VMEM((8192, 256), BF16),
            pltpu.VMEM((64, 8192), BF16),
            pltpu.VMEM((2, 4, 2, 2, 2, 2, 128, 128), BF16),
            pltpu.VMEM((4, 256, 64), BF16),
            pltpu.VMEM((256, 64), F32),
            pltpu.VMEM((256, 256), F32),
            pltpu.VMEM((256, 256), F32),
            pltpu.VMEM((256, 64), F32),
            pltpu.VMEM((2, 256, 128), BF16),
            dma((3,)), dma((2,)),
            dma((4, 4)), dma((4, 4)), dma((4, 5)), dma((4, 5)),
            dma((4, 4)), dma((4, 4)), dma((4, 5)), dma((4, 5)),
            dma((3,)), dma((3,)), dma((2, 4)),
        ],
        compiler_params=pltpu.CompilerParams(
            collective_id=0, has_side_effects=True, vmem_limit_bytes=VMEM_MAX
        ),
        name="front",
    )(tokens, gain, wq, kp, vp, cosf, sinf)


NG = 8


def cache_kernel(
    mask, q_hbm, k_hbm, v_hbm, o_hbm, lse,
    q, kraw, vraw, kt, vt, sbuf, mx, ls, acc, lev, obuf, listed, count,
    qsem, ksem, vsem, osem,
):
    qcopy = pltpu.make_async_copy(q_hbm, q, qsem.at[0])
    chunk = 256
    loads = []
    for i in range(8):
        r = pl.ds(i * chunk, chunk)
        kc = pltpu.make_async_copy(k_hbm.at[r], kraw.at[r], ksem.at[i])
        vc = pltpu.make_async_copy(v_hbm.at[r], vraw.at[r], vsem.at[i])
        kc.start()
        vc.start()
        loads.append((kc, vc))
    qcopy.start()

    @pl.loop(0, 8)
    def _(b):
        def put(k, n):
            listed[b, n] = k
            return n + jnp.where(mask[b, k] > 0, 1, 0)

        count[b] = lax.fori_loop(0, 16, put, 0)

    for i in range(8):
        kc, vc = loads[i]
        kc.wait()

        @pl.loop(0, chunk // 64)
        def _(t):
            r = pl.ds(pl.multiple_of(i * chunk + t * 64, 64), 64)
            kt[:, r, :] = jnp.swapaxes(kraw[r], 0, 1)

        vc.wait()

        @pl.loop(0, chunk // 128)
        def _(t):
            r = pl.ds(pl.multiple_of(i * chunk + t * 128, 128), 128)
            vt[:, :, r] = jnp.swapaxes(jnp.swapaxes(vraw[r], 0, 1), 1, 2)

    qcopy.wait()

    def folded(v, op):
        return op(v.reshape(v.shape[0] // 8, 8, 256), axis=0)

    @pl.loop(0, 8 // NG)
    def _(gp):
        gammas = []
        for e in range(NG):
            gamma = gp * NG + e
            yb = gamma // 2
            gammas.append((gamma, 2 * (yb ^ (yb >> 1)) + lax.rem(gamma, 2)))

        @pl.loop(0, 8)
        def _(b):
            u = b // 4
            rows = pl.ds(pl.multiple_of(lax.rem(b, 4) * 32, 32), 32)
            n = count[b]
            pairs = n // 2
            qs = []
            for e, (gamma, g) in enumerate(gammas):
                qs.append(q[:, :, u, pl.ds(2 * gamma, 2), rows, :].reshape(256, 128))
                mx[e] = jnp.full((8, 256), NEG, F32)
                ls[e] = jnp.zeros((8, 256), F32)
                acc[e] = jnp.zeros((128, 256), F32)

            def at(k):
                return pl.ds(pl.multiple_of(listed[b, k] * 128, 128), 128)

            def score(kk, qq):
                return lax.dot_general(kk, qq, (((1,), (1,)), ((), ())), preferred_element_type=F32)

            @pl.loop(0, pairs)
            def _(i):
                r0, r1 = at(2 * i), at(2 * i + 1)
                for e, (gamma, g) in enumerate(gammas):
                    sc = score(jnp.concatenate([kt[g, r0, :], kt[g, r1, :]], axis=0), qs[e])
                    sbuf[e, i] = sc
                    mx[e] = jnp.maximum(mx[e], folded(sc, jnp.max))

            @pl.when(lax.rem(n, 2) == 1)
            def _():
                r0 = at(n - 1)
                for e, (gamma, g) in enumerate(gammas):
                    sc = score(kt[g, r0, :], qs[e])
                    sbuf[e, pairs, 0:128, :] = sc
                    mx[e] = jnp.maximum(mx[e], folded(sc, jnp.max))

            tops = [jnp.max(mx[e], axis=0, keepdims=True) * SCALE2 for e in range(NG)]

            @pl.loop(0, pairs)
            def _(i):
                r0, r1 = at(2 * i), at(2 * i + 1)
                for e, (gamma, g) in enumerate(gammas):
                    w = jnp.exp2(sbuf[e, i] * SCALE2 - tops[e])
                    ls[e] += folded(w, jnp.sum)
                    vv = jnp.concatenate([vt[g, :, r0], vt[g, :, r1]], axis=1)
                    acc[e] += jnp.dot(vv, w.astype(BF16), preferred_element_type=F32)

            @pl.when(lax.rem(n, 2) == 1)
            def _():
                r0 = at(n - 1)
                for e, (gamma, g) in enumerate(gammas):
                    w = jnp.exp2(sbuf[e, pairs, 0:128, :] * SCALE2 - tops[e])
                    ls[e] += folded(w, jnp.sum)
                    acc[e] += jnp.dot(vt[g, :, r0], w.astype(BF16), preferred_element_type=F32)

            for e, (gamma, g) in enumerate(gammas):
                total = jnp.sum(ls[e], axis=0, keepdims=True)
                safe = jnp.where(total > 0.0, total, 1.0)
                out = (acc[e] * (1.0 / safe)).T.astype(BF16)
                obuf[:, :, u, pl.ds(2 * gamma, 2), rows, :] = out.reshape(2, 2, 2, 32, 128)
                lev[b, pl.ds(gamma, 1), :] = jnp.where(total > 0.0, tops[e] + jnp.log2(safe), NEG)

    outs = []
    for cc in range(2):
        c = pltpu.make_async_copy(obuf.at[cc], o_hbm.at[cc], osem.at[cc])
        c.start()
        outs.append(c)
    lane = lax.broadcasted_iota(jnp.int32, (32, 128), 1)

    @pl.loop(0, 8)
    def _(b):
        rows = pl.ds(pl.multiple_of(lax.rem(b, 4) * 32, 32), 32)
        turned = jnp.concatenate([lev[b], jnp.zeros((120, 256), F32)], axis=0).T
        for m in range(4):
            first = turned[64 * m : 64 * m + 32]
            second = pltpu.roll(turned[64 * m + 32 : 64 * m + 64], 8, 1)
            lse[m // 2, m % 2, b // 4, rows, :] = jnp.where(lane < 8, first, second)

    for c in outs:
        c.wait()


def cache_attention(mask, q, k, v):
    any_spec = pl.BlockSpec(memory_space=pl.ANY)
    vmem = pl.BlockSpec(memory_space=pltpu.VMEM)
    dma = pltpu.SemaphoreType.DMA
    shape = (2, 2, 2, 16, 128, 128)
    return pl.pallas_call(
        cache_kernel,
        out_shape=(
            jax.ShapeDtypeStruct(shape, BF16),
            jax.ShapeDtypeStruct((2, 2, 2, 128, 128), F32),
        ),
        in_specs=[pl.BlockSpec(memory_space=pltpu.SMEM), any_spec, any_spec, any_spec],
        out_specs=(any_spec, vmem),
        scratch_shapes=[
            pltpu.VMEM(shape, BF16),
            pltpu.VMEM((2048, 8, 128), BF16),
            pltpu.VMEM((2048, 8, 128), BF16),
            pltpu.VMEM((8, 2048, 128), BF16),
            pltpu.VMEM((8, 128, 2048), BF16),
            pltpu.VMEM((NG, 8, 256, 256), F32),
            pltpu.VMEM((NG, 8, 256), F32),
            pltpu.VMEM((NG, 8, 256), F32),
            pltpu.VMEM((NG, 128, 256), F32),
            pltpu.VMEM((8, 8, 256), F32),
            pltpu.VMEM(shape, BF16),
            pltpu.SMEM((8, 17), jnp.int32),
            pltpu.SMEM((8,), jnp.int32),
            dma((1,)), dma((8,)), dma((8,)), dma((2,)),
        ],
        compiler_params=pltpu.CompilerParams(vmem_limit_bytes=VMEM_MAX),
        name="cache",
    )(mask, q, k, v)


def blend(a, b):
    wa = 1.0 / (1.0 + jnp.exp2(b - a))
    wb = 1.0 / (1.0 + jnp.exp2(a - b))
    level = jnp.maximum(a, b) + jnp.log2(1.0 + jnp.exp2(-jnp.abs(a - b)))
    return wa, wb, level


def columns(rows):
    stacked = jnp.concatenate(rows, axis=0) if len(rows) > 1 else rows[0]
    fill = jnp.zeros((128 - len(rows), 128), F32)
    return jnp.concatenate([stacked, fill], axis=0).T


def back_kernel(
    o_hbm, lse, self_o, self_l, w_out, tok, out,
    ob, oc, lsec, acc, lrow, snd0, snd1, snd2, snd3, rcv0, rcv1, rcv2, rcv3,
    rl0, rl1, rl2, rl3, sl0, sl1, sl2, sl3, att, wbuf, ysend, yrecv, yacc, tokp, res, hout,
    ys0, ys1, ys2, ys3, yr0, yr1, yr2, yr3,
    wsem, obsem, ocs, ocr, lss, lsr, tsem, ss, rs, ls_, lr_, ycs, ycr, yss, yrs, hss, hrs,
):
    core, bits, dims, partner, _, _ = place()
    section = lax.axis_index("section")
    rank = lax.axis_index("seq")
    chip = rank // 2
    up = lax.rem(section + 1, 4)
    down = lax.rem(section + 3, 4)
    load_w = pltpu.make_async_copy(w_out, wbuf, wsem.at[0])
    own_loads = []
    for p in range(4):
        c = pltpu.make_async_copy(o_hbm.at[core, p], ob.at[p], obsem.at[p])
        c.start()
        own_loads.append(c)
    load_w.start()
    targets = [{"seq": t} for t in (partner,) + dims]
    for sec in (up, down):
        for cc in range(2):
            targets.append({"section": sec, "seq": chip * 2 + cc})
    greet(targets)
    waits = []
    lcopy = push(lse.at[1 - core], lsec, lss.at[0], lsr.at[0], {"seq": partner})
    lcopy.start()
    ocopies = []
    for p in range(4):
        c = push(o_hbm.at[1 - core, p], oc.at[p], ocs.at[p], ocr.at[p], {"seq": partner})
        c.start()
        ocopies.append(c)
    tcopy = push(
        tok.at[:, pl.ds(pl.multiple_of((1 - core) * 4096, 4096), 4096)], tokp, tsem.at[0], tsem.at[1], {"seq": partner}
    )
    tcopy.start()
    waits += ocopies + [lcopy, tcopy]

    snd = (snd0, snd1, snd2, snd3)
    rcv = (rcv0, rcv1, rcv2, rcv3)
    rl = (rl0, rl1, rl2, rl3)
    sl = (sl0, sl1, sl2, sl3)
    lcopy.wait_recv()
    done = [[] for _ in range(4)]
    flight = [None] * 4

    def remaining(p):
        return [d for d in range(4) if d not in done[p]]

    def start_step(p, s):
        d = (p + s) % 4
        rest = [k for k in remaining(p) if k != d]
        for i, idx in enumerate(blocks(bits, rest, (d,))):
            snd[s][p, i] = acc[(p,) + idx].astype(BF16)
            sl[s][p, i] = lrow[(p,) + idx]
        c1 = push(snd[s].at[p], rcv[s].at[p], ss.at[p, s], rs.at[p, s], {"seq": dims[d]})
        c2 = push(sl[s].at[p], rl[s].at[p], ls_.at[p, s], lr_.at[p, s], {"seq": dims[d]})
        c2.start()
        c1.start()
        done[p].append(d)
        flight[p] = (c1, c2)
        waits.extend((c1, c2))

    for s in range(5):
        for p in range(4):
            if s == 0:
                own_loads[p].wait()
                ocopies[p].wait_recv()
                wa, wb, level = blend(lse[core, p], lsec[p])
                turned = level.T
                for b in range(16):
                    sb = static_bits(b)
                    t = (b % 2) * 8 + b // 2
                    acc[(p,) + sb] = (
                        ob[(p,) + sb].astype(F32) * wa[:, t : t + 1]
                        + oc[(p,) + sb].astype(F32) * wb[:, t : t + 1]
                    )
                    lrow[(p,) + sb] = turned[t : t + 1, :]
            else:
                c1, c2 = flight[p]
                c2.wait_recv()
                c1.wait_recv()
                keep = blocks(bits, remaining(p))
                n = len(keep)
                got = rl[s - 1][p].reshape(n, 1, 128)
                a_rows = [lrow[(p,) + idx] for idx in keep]
                wa_rows, wb_rows = [], []
                for i, idx in enumerate(keep):
                    wa, wb, level = blend(a_rows[i], got[i])
                    wa_rows.append(wa)
                    wb_rows.append(wb)
                    lrow[(p,) + idx] = level
                wac, wbc = columns(wa_rows), columns(wb_rows)
                for i, idx in enumerate(keep):
                    acc[(p,) + idx] = (
                        acc[(p,) + idx] * wac[:, i : i + 1]
                        + rcv[s - 1][p, i].astype(F32) * wbc[:, i : i + 1]
                    )
            if s < 4:
                start_step(p, s)

    me = (bits[3], bits[2], bits[1], bits[0])
    for p in range(4):
        j, u = p // 2, p % 2
        level = jnp.broadcast_to(lrow[(p,) + me], (128, 128)).T
        mine = self_l[j, 128 * u : 128 * (u + 1), :]
        wa, wb, _ = blend(level, mine)
        merged = acc[(p,) + me] * wa + self_o[j, 128 * u : 128 * (u + 1), :] * wb
        att[128 * u : 128 * (u + 1), 128 * j : 128 * (j + 1)] = merged.astype(BF16)
    load_w.wait()

    def cols(half, p):
        return pl.ds(pl.multiple_of(half * 4096 + p * 1024, 1024), 1024)

    @pl.loop(0, 4)
    def _(p):
        r = jnp.dot(att[...], wbuf[:, cols(1 - core, p)], preferred_element_type=F32).astype(BF16)
        for b in range(16):
            n = natural_chip(b)
            ysend[(p,) + static_bits(b)] = r[16 * n : 16 * n + 16, :]
        push(ysend.at[p], yrecv.at[p], ycs.at[p], ycr.at[p], {"seq": partner}).start()

    @pl.loop(0, 4)
    def _(p):
        r = jnp.dot(att[...], wbuf[:, cols(core, p)], preferred_element_type=F32)
        for b in range(16):
            n = natural_chip(b)
            yacc[(p,) + static_bits(b)] = r[16 * n : 16 * n + 16, :]

    ys = (ys0, ys1, ys2, ys3)
    yr = (yr0, yr1, yr2, yr3)
    done = [[] for _ in range(4)]
    for s in range(5):
        for p in range(4):
            if s == 0:
                c = push(ysend.at[p], yrecv.at[p], ycs.at[p], ycr.at[p], {"seq": partner})
                waits.append(c)
                c.wait_recv()
                for b in range(16):
                    sb = static_bits(b)
                    yacc[(p,) + sb] += yrecv[(p,) + sb].astype(F32)
            else:
                flight[p].wait_recv()
                for i, idx in enumerate(blocks(bits, remaining(p))):
                    yacc[(p,) + idx] += yr[s - 1][p, i].astype(F32)
            if s < 4:
                d = (p + s) % 4
                rest = [k for k in remaining(p) if k != d]
                for i, idx in enumerate(blocks(bits, rest, (d,))):
                    ys[s][p, i] = yacc[(p,) + idx].astype(BF16)
                c = push(ys[s].at[p], yr[s].at[p], yss.at[p, s], yrs.at[p, s], {"seq": dims[d]})
                c.start()
                done[p].append(d)
                flight[p] = c
                waits.append(c)

    tcopy.wait_recv()
    mine = tok[:, pl.ds(pl.multiple_of(core * 4096, 4096), 4096)].astype(F32)
    other = tokp[...].astype(F32)
    low = jnp.where(core == 0, mine, other)
    high = jnp.where(core == 0, other, mine)
    for p in range(4):
        total = yacc[(p,) + me]
        span = slice(1024 * p, 1024 * (p + 1))
        res[0, :, span] = (low[:, span] + total[0:8]).astype(BF16)
        res[1, :, span] = (high[:, span] + total[8:16]).astype(BF16)
    final = []
    for cc in range(2):
        c = push(
            res.at[cc], hout.at[core], hss.at[cc], hrs.at[core], {"section": up, "seq": chip * 2 + cc},
        )
        c.start()
        waits.append(c)
    for cc in range(2):
        push(
            res.at[cc], hout.at[cc], hss.at[cc], hrs.at[cc], {"section": up, "seq": chip * 2 + cc},
        ).wait_recv()
        out[:, 4096 * cc : 4096 * (cc + 1)] = hout[cc]
    for c in waits:
        c.wait_send()


def back(o, lse, self_o, self_l, w_out, tokens):
    any_spec = pl.BlockSpec(memory_space=pl.ANY)
    vmem = pl.BlockSpec(memory_space=pltpu.VMEM)
    dma = pltpu.SemaphoreType.DMA
    bit = (2, 2, 2, 2)
    steps = (8, 4, 2, 1)
    scratch = [
        pltpu.VMEM((4,) + bit + (128, 128), BF16),
        pltpu.VMEM((4,) + bit + (128, 128), BF16),
        pltpu.VMEM((4, 128, 128), F32),
        pltpu.VMEM((4,) + bit + (128, 128), F32),
        pltpu.VMEM((4,) + bit + (1, 128), F32),
    ]
    scratch += [pltpu.VMEM((4, n, 128, 128), BF16) for n in steps]
    scratch += [pltpu.VMEM((4, n, 128, 128), BF16) for n in steps]
    scratch += [pltpu.VMEM((4, n, 1, 128), F32) for n in steps + steps]
    scratch += [
        pltpu.VMEM((256, 256), BF16),
        pltpu.VMEM((256, 8192), BF16),
        pltpu.VMEM((4,) + bit + (16, 1024), BF16),
        pltpu.VMEM((4,) + bit + (16, 1024), BF16),
        pltpu.VMEM((4,) + bit + (16, 1024), F32),
        pltpu.VMEM((8, 4096), BF16),
        pltpu.VMEM((2, 8, 4096), BF16),
        pltpu.VMEM((2, 8, 4096), BF16),
    ]
    scratch += [pltpu.VMEM((4, n, 16, 1024), BF16) for n in steps]
    scratch += [pltpu.VMEM((4, n, 16, 1024), BF16) for n in steps]
    scratch += [
        dma((1,)), dma((4,)), dma((4,)), dma((4,)), dma((1,)), dma((1,)), dma((2,)),
        dma((4, 4)), dma((4, 4)), dma((4, 4)), dma((4, 4)),
        dma((4,)), dma((4,)), dma((4, 4)), dma((4, 4)), dma((2,)), dma((2,)),
    ]
    return pl.pallas_call(
        back_kernel,
        out_shape=jax.ShapeDtypeStruct((8, 8192), BF16),
        in_specs=[any_spec, vmem, vmem, vmem, any_spec, vmem],
        out_specs=vmem,
        scratch_shapes=scratch,
        compiler_params=pltpu.CompilerParams(
            collective_id=1, has_side_effects=True, vmem_limit_bytes=VMEM_MAX
        ),
        name="back",
    )(o, lse, self_o, self_l, w_out, tokens)


def on_device(
    tokens, norm_gain, w_query, key_projection, value_projection, w_out,
    key_cache, cached_value_rows, cache_mask, span_offset,
):
    offset = span_offset[0].astype(F32)
    positions = offset + jnp.arange(256, dtype=jnp.int32).astype(F32)
    freqs = ROPE_BASE ** (-2.0 * jnp.arange(64, dtype=F32) / 128)
    angles = positions[:, None] * freqs[None, :]
    cosine, sine = jnp.cos(angles), jnp.sin(angles)
    cosf = jnp.concatenate([cosine, cosine], axis=1)
    sinf = jnp.concatenate([-sine, sine], axis=1)
    q, self_o, self_l = front(
        tokens[0], norm_gain, w_query[0], key_projection[0].T, value_projection[0].T, cosf, sinf
    )
    o, lse = cache_attention(
        cache_mask[0], q.reshape(2, 2, 2, 16, 128, 128), key_cache[0], cached_value_rows[0]
    )
    bit = (2, 2, 2, 2)
    handed = back(
        o.reshape((2, 4) + bit + (128, 128)), lse.reshape(2, 4, 128, 128), self_o, self_l, w_out[0], tokens[0]
    )
    return handed[None]


def solution(mesh):
    placed = (
        P("section", "seq", None),
        P("section", None),
        P("section", None, "seq"),
        P("section", None, "seq"),
        P("section", None, "seq"),
        P("section", "seq", None),
        P("section", "seq", None, None),
        P("section", "seq", None, None),
        P("section", None, "seq"),
        P("section"),
    )
    return jax.shard_map(
        on_device, mesh=mesh, in_specs=placed, out_specs=P("section", "seq", None), check_vma=False
    )
```
